32 devices in a mesh: samp: 8 (over z, x), snp: 4 (over y, core).
Axes of the slice: x: 2, y: 2, z: 4, core: 2. Of those that a mesh axis runs over, the one named last changes fastest.
Arguments:
- genotype: bfloat16 [16384, 1024], P('samp', 'snp'), may hold values from -60 to 60
- phenotype: float32 [16384], P('samp'), may hold values from -6 to 6
- residual: float32 [16384], P('samp'), may hold values from -6 to 6
- sign_flips: int32 [16384, 127], P('samp'), may hold values from -1 to 1, as said below
- weights: bfloat16 [128, 49, 128], P('snp'), may hold values from -0.5 to 0.5
- member: int32 [128, 49], P('snp'), may hold values 0 or 1
- gene_start: int32 [128], P('snp'), may hold values from 0 to 1023, as said below
- gene_end: int32 [128], P('snp'), may hold values from 1 to 1024, as said below
Outputs:
- z_scores: float32 [128, 49, 128], P('snp')
The draws below stay inside these ranges and needn't reach their ends.
Inputs may be any that keep to these rules, and one draw needn't show every extreme that they name: `sign_flips`: each entry is -1 or 1. `gene_start`: gene g's start lies among the SNPs of block g // 32 of 256 SNPs, at or past (g % 32) * (8) within it and before the next such mark, except that the last gene starts at 1023; the first gene starts at 0. gene_end - gene_start lies between 1 and 128 and reaches 128 in every block of genes except possibly the last; gene_end is at most 1024, and the last gene ends at 1024.
All inputs are finite; a program needn't handle non-finite values. No bound on the sum of `member` on one device may be relied on, other than what follows from the above.
Results may differ from the reference program's by a relative error of at most 0.0041.
Values may be sent and summed in bfloat16 or wider, within the bound.
A program may use at most 64 MiB of HBM per device.

```python
import jax
import jax.numpy as jnp
from jax import lax

SNP_DEV = 256
GENE_DEV = 32
WIN = 128
TISSUE = 49
FLIPS = 127
SAMPLES = 16384
SNPS = 1024
GENES = 128


def draw_genotype(key, part):
    key_base, key_row, key_col = jax.random.split(key, 3)
    row_pos = jnp.arange(SAMPLES, dtype=jnp.float32)[:, None] / (SAMPLES - 1)
    row_scale = 10.0 ** jax.random.uniform(key_row, (SAMPLES, 1)) * (1.0 + 2.0 * row_pos)
    col_scale = 0.5 + 1.5 * jax.random.uniform(key_col, (1, SNPS))
    values = jnp.clip(jax.random.normal(key_base, (SAMPLES, SNPS)), -4.0, 4.0)
    return (0.2 * values * row_scale * col_scale).astype(jnp.bfloat16)


def draw_sign_flips(key, part):
    coins = jax.random.randint(jax.random.fold_in(key, 3), (SAMPLES, FLIPS), 0, 2)
    return (2 * coins - 1).astype(jnp.int32)


def gene_windows(key):
    key_place, key_span = jax.random.split(jax.random.fold_in(key, 11), 2)
    spacing = SNP_DEV // GENE_DEV
    gene_ids = jnp.arange(GENES, dtype=jnp.int32)
    block_index = gene_ids // GENE_DEV
    slot_index = gene_ids % GENE_DEV
    first_snp = block_index * SNP_DEV + slot_index * spacing + jax.random.randint(key_place, (GENES,), 0, spacing)
    first_snp = jnp.where(gene_ids == 0, 0, first_snp)
    first_snp = jnp.where(gene_ids == GENES - 1, SNPS - 1, first_snp)
    length = jax.random.randint(key_span, (GENES,), WIN // 4, WIN + 1)
    length = jnp.where(slot_index == GENE_DEV - 1, WIN, length)
    last_snp = jnp.minimum(first_snp + length, SNPS)
    return (first_snp.astype(jnp.int32), last_snp.astype(jnp.int32))


def draw_gene_start(key, part):
    return gene_windows(key)[0]


def draw_gene_end(key, part):
    return gene_windows(key)[1]


def with_ends(drawn, rng, least, top_value):
    shape = drawn.shape
    place = [jax.random.randint(jax.random.fold_in(rng, axis), (), 0, shape[axis]) for axis in range(len(shape))]
    drawn = drawn.at[tuple(place)].set(least)
    longest = shape.index(max(shape))
    place[longest] = (place[longest] + 1) % shape[longest]
    return drawn.at[tuple(place)].set(top_value)


def steps_of(own_key, dims, cuts, low, top_value):
    level, own = 1.0, jax.random.fold_in(own_key, 6)
    for position, shards_of in cuts:
        heights = jnp.exp(jax.random.uniform(jax.random.fold_in(own, position), (shards_of,), jnp.float32, low / len(cuts), top_value / len(cuts)))
        level = level * jnp.repeat(heights, dims[position] // shards_of).reshape([-1 if axis == position else 1 for axis in range(len(dims))])
    return level


def noise(stream_key, extent, scale, limit, cuts=(), kind=jnp.bfloat16):
    drawn = scale * jax.random.normal(stream_key, extent, jnp.float32)
    if cuts:
        drawn = drawn * steps_of(stream_key, extent, cuts, -0.22, 0.18)
    return jnp.clip(drawn, -limit, limit).astype(kind)


def setup_inputs(seed: int = 0) -> dict:
    arg_keys = jax.random.split(jax.random.key(seed), 9)
    genotype = draw_genotype(jax.random.fold_in(arg_keys[8], 71), 0)
    phenotype = noise(arg_keys[1], (SAMPLES,), 1.0, 6.0, ((0, 8),), jnp.float32)
    residual = noise(arg_keys[2], (SAMPLES,), 1.0, 6.0, ((0, 8),), jnp.float32)
    sign_flips = draw_sign_flips(jax.random.fold_in(arg_keys[8], 71), 0)
    weights = noise(arg_keys[4], (GENES, TISSUE, WIN), WIN ** -0.5, 0.5, ((0, 4),))
    member = with_ends((jax.random.randint(arg_keys[5], (GENES, TISSUE), 0, 4) < 3).astype(jnp.int32), jax.random.fold_in(arg_keys[5], 1), 0, 1)
    gene_start = draw_gene_start(jax.random.fold_in(arg_keys[8], 71), 0)
    gene_end = draw_gene_end(jax.random.fold_in(arg_keys[8], 71), 0)
    return {"genotype": genotype, "phenotype": phenotype, "residual": residual, "sign_flips": sign_flips, "weights": weights, "member": member, "gene_start": gene_start, "gene_end": gene_end}


def reference(genotype, phenotype, residual, sign_flips, weights, member, gene_start, gene_end):
    sample_total = genotype.shape[0]
    padded = jnp.pad(genotype, ((0, 0), (0, WIN)))
    labels = jnp.concatenate([phenotype[:, None], residual[:, None] * sign_flips.astype(jnp.float32)], axis=1)
    labels = lax.optimization_barrier(labels.astype(jnp.bfloat16)).astype(jnp.float32)
    sum_lab = lax.optimization_barrier(jnp.sum(labels, axis=0))
    window_pos = jnp.arange(WIN, dtype=jnp.int32)
    scale_root = jnp.sqrt(jnp.asarray(sample_total, dtype=jnp.float32))

    def one_gene(items):
        gene_wts, gene_mem, gene_first, gene_last = items
        window = lax.dynamic_slice_in_dim(padded, gene_first.astype(jnp.int32), WIN, 1).astype(jnp.float32)
        inside_mask = (window_pos < gene_last - gene_first).astype(jnp.float32)
        window_wts = gene_wts.astype(jnp.float32) * gene_mem.astype(jnp.float32)[:, None] * inside_mask[None, :]
        predicted = jnp.dot(window, window_wts.T, precision=lax.Precision.HIGHEST)
        predicted = lax.optimization_barrier(predicted.astype(jnp.bfloat16)).astype(jnp.float32)
        sum_pred = lax.optimization_barrier(jnp.sum(predicted, axis=0))
        sum_sq = lax.optimization_barrier(jnp.sum(predicted * predicted, axis=0))
        cross_prod = jnp.dot(predicted.T, labels, precision=lax.Precision.HIGHEST)
        col_mean = sum_pred / sample_total
        col_spread = jnp.sqrt(sum_sq / sample_total - col_mean * col_mean + 1e-06)
        return (cross_prod - col_mean[:, None] * sum_lab[None, :]) / (col_spread[:, None] * scale_root)
    return lax.map(one_gene, (weights, member, gene_start, gene_end))
```

```python
import functools

import jax
import jax.numpy as jnp
from jax import lax
from jax.experimental import pallas as pl
from jax.experimental.pallas import tpu as pltpu
from jax.sharding import PartitionSpec as P

MESH = pl.DeviceIdType.MESH
TILE = 16
PARTS = 4


def across(left, right):
    return lax.dot_general(left, right, (((0,), (0,)), ((), ())), preferred_element_type=jnp.float32)


def iotas(rows, cols):
    return (
        lax.broadcasted_iota(jnp.int32, (rows, cols), 0),
        lax.broadcasted_iota(jnp.int32, (rows, cols), 1),
    )


def share_of(rows, count):
    per = -(-rows // (count * TILE)) * TILE
    while rows % per:
        per += TILE
    return per


def columns_of(rows_ref):
    tiles, width = rows_ref.shape
    block = rows_ref[...]
    if tiles < width:
        block = jnp.concatenate([block, jnp.zeros((width - tiles, width), jnp.float32)], axis=0)
    return block.T


def sums_kernel(
    count, ring, window,
    geno, phen, resid, flips,
    near_out, far_out, sums_out,
    geno_v, flips_v, halo_v, labels_v,
    early_s, early_r, early_p, early_g,
    late_s, late_r, late_p, late_g,
    tail_v, tail_sums, sums_s, sums_r, sums_t,
    load_sem, flip_sem, halo_ss, halo_rs,
    es_ss, es_rs, eg_ss, eg_rs, ls_ss, ls_rs, lg_ss, lg_rs,
    sm_ss, sm_rs, tl_ss, tl_rs,
):
    me = lax.axis_index("samp")
    mine = lax.axis_index("snp")
    before = lax.rem(mine + ring - 1, ring)
    after = lax.rem(mine + 1, ring)
    samples, snps = geno_v.shape
    blocks = snps // window
    part = samples // PARTS

    loads, flip_loads = [], []
    for i in range(PARTS):
        rows = pl.ds(i * part, part)
        loads.append(pltpu.make_async_copy(geno.at[rows], geno_v.at[rows], load_sem.at[i]))
        flip_loads.append(pltpu.make_async_copy(flips.at[rows], flips_v.at[rows], flip_sem.at[i]))
        loads[i].start()
        flip_loads[i].start()

    def peers(body):
        if count <= 16:
            for dist in range(1, count):
                body(dist)
        else:
            def step(dist, carry):
                body(dist)
                return carry
            lax.fori_loop(1, count, step, 0)

    def ahead(dist):
        return lax.rem(me + dist, count)

    def behind(dist):
        return lax.rem(me + count - dist, count)

    barrier = pltpu.get_barrier_semaphore()
    peers(lambda dist: pl.semaphore_signal(
        barrier, inc=1, device_id=(ahead(dist), mine), device_id_type=MESH))
    for other in (before, after):
        pl.semaphore_signal(barrier, inc=1, device_id=(me, other), device_id_type=MESH)
    pl.semaphore_wait(barrier, count + 1)

    def remote(src, dst, ss, rs, device):
        return pltpu.make_async_remote_copy(
            src_ref=src, dst_ref=dst, send_sem=ss, recv_sem=rs,
            device_id=device, device_id_type=MESH)

    halos = []
    for i in range(PARTS):
        rows = pl.ds(i * part, part)
        halos.append(remote(
            geno.at[rows, pl.ds(0, window)], halo_v.at[rows],
            halo_ss.at[i], halo_rs.at[i], (me, before)))
        halos[i].start()

    def guarded(owners, index, body):
        if owners == count:
            body()
        else:
            pl.when(index < owners)(body)

    def scatter_copy(buf, got, ss, rs, per, dist):
        start = pl.multiple_of(ahead(dist) * per, TILE)
        return remote(buf.at[pl.ds(start, per)], got.at[dist], ss.at[dist], rs.at[dist], (ahead(dist), mine))

    def gather_copy(piece, full, ss, rs, per, dist):
        start = pl.multiple_of(me * per, TILE)
        return remote(piece, full.at[pl.ds(start, per)], ss.at[dist], rs.at[dist], (ahead(dist), mine))

    def scatter_start(buf, got, ss, rs, per):
        owners = buf.shape[0] // per
        peers(lambda dist: guarded(
            owners, ahead(dist), lambda: scatter_copy(buf, got, ss, rs, per, dist).start()))

    def reduce_and_gather(buf, got, piece, full, ss, rs, gss, grs, per):
        owners = buf.shape[0] // per

        def owner():
            start = pl.multiple_of(me * per, TILE)
            rows = pl.ds(start, per)
            total = buf[rows, :].astype(jnp.float32)
            if count <= 16:
                for dist in range(1, count):
                    scatter_copy(buf, got, ss, rs, per, dist).wait_recv()
                    total += got[dist].astype(jnp.float32)
            else:
                def step(dist, total):
                    scatter_copy(buf, got, ss, rs, per, dist).wait_recv()
                    return total + got[dist].astype(jnp.float32)
                total = lax.fori_loop(1, count, step, total)
            piece[...] = total.astype(piece.dtype)
            peers(lambda dist: gather_copy(piece, full, gss, grs, per, dist).start())
            full[rows, :] = piece[...]
        guarded(owners, me, owner)

    def gather_wait(buf, piece, full, gss, grs, per):
        owners = buf.shape[0] // per

        def one(dist):
            start = pl.multiple_of(behind(dist) * per, TILE)
            guarded(owners, behind(dist), lambda: remote(
                piece, full.at[pl.ds(start, per)], gss.at[dist], grs.at[dist], (ahead(dist), mine)).wait_recv())
        peers(one)

    def sends_wait(buf, got, piece, full, ss, rs, gss, grs, per):
        owners = buf.shape[0] // per
        peers(lambda dist: guarded(
            owners, ahead(dist), lambda: scatter_copy(buf, got, ss, rs, per, dist).wait_send()))
        guarded(owners, me, lambda: peers(
            lambda dist: gather_copy(piece, full, gss, grs, per, dist).wait_send()))

    flip_count = flips_v.shape[1]
    phen_cols = columns_of(phen)
    resid_cols = columns_of(resid)
    lanes = phen.shape[1]
    for i in range(PARTS):
        flip_loads[i].wait()
        for t in range(i * part // lanes, (i + 1) * part // lanes):
            rows = pl.ds(t * lanes, lanes)
            signs = flips_v[rows, :].astype(jnp.float32)
            labels_v[rows, pl.ds(0, flip_count)] = (signs * resid_cols[:, t:t + 1]).astype(jnp.bfloat16)
            labels_v[rows, pl.ds(flip_count, 1)] = phen_cols[:, t:t + 1].astype(jnp.bfloat16)

    for i in range(PARTS):
        loads[i].wait()
    own = geno_v[...]
    labels = labels_v[...]
    with_labels = across(own, labels)
    gram = across(own, own)
    ones = jnp.ones((8, samples), jnp.bfloat16)
    col_sums = jnp.dot(ones, own, preferred_element_type=jnp.float32)
    lab_sums = jnp.dot(ones, labels, preferred_element_type=jnp.float32)
    row8, _ = iotas(8, window)
    sums = jnp.where(row8 == blocks, lab_sums, 0.0)
    for b in range(blocks):
        sums = jnp.where(row8 == b, col_sums[:, b * window:(b + 1) * window], sums)
    sums_s[...] = sums

    def sums_copy(dist):
        return remote(sums_s, sums_r.at[dist], sm_ss.at[dist], sm_rs.at[dist], (ahead(dist), mine))

    row, col = iotas(window, window)
    early_s[pl.ds(0, window), :] = with_labels[0:window].astype(jnp.bfloat16)
    for b in range(blocks - 1):
        low, mid, high = b * window, (b + 1) * window, (b + 2) * window
        band = jnp.where(col >= row, gram[low:mid, low:mid], gram[low:mid, mid:high])
        early_s[pl.ds((1 + b) * window, window), :] = band.astype(jnp.bfloat16)
        early_s[pl.ds((blocks + b) * window, window), :] = with_labels[mid:high].astype(jnp.bfloat16)
    early_per, late_per = early_p.shape[0], late_p.shape[0]
    scatter_start(early_s, early_r, es_ss, es_rs, early_per)
    peers(lambda dist: sums_copy(dist).start())

    last = snps - window
    with_halo = jnp.zeros((window, window), jnp.float32)
    for i in range(PARTS):
        rows = pl.ds(i * part, part)
        halos[i].wait_recv()
        with_halo += across(geno_v[rows, pl.ds(last, window)], halo_v[rows, :])
    late_s[...] = jnp.where(col >= row, gram[last:, last:], with_halo).astype(jnp.bfloat16)
    scatter_start(late_s, late_r, ls_ss, ls_rs, late_per)

    reduce_and_gather(early_s, early_r, early_p, early_g, es_ss, es_rs, eg_ss, eg_rs, early_per)

    sums_total = sums_s[...]
    if count <= 16:
        for dist in range(1, count):
            sums_copy(dist).wait_recv()
            sums_total += sums_r[dist]
    else:
        def step(dist, total):
            sums_copy(dist).wait_recv()
            return total + sums_r[dist]
        sums_total = lax.fori_loop(1, count, step, sums_total)
    sums_t[...] = sums_total
    tail_copies = [remote(sums_t, tail_sums, tl_ss.at[0], tl_rs.at[0], (me, before))]
    tail_copies[0].start()

    reduce_and_gather(late_s, late_r, late_p, late_g, ls_ss, ls_rs, lg_ss, lg_rs, late_per)

    gather_wait(early_s, early_p, early_g, eg_ss, eg_rs, early_per)
    tail_copies.append(remote(
        early_g.at[pl.ds(0, 2 * window)], tail_v, tl_ss.at[1], tl_rs.at[1], (me, before)))
    tail_copies[1].start()
    near_out[pl.ds(0, early_g.shape[0]), :] = early_g[...]
    gather_wait(late_s, late_p, late_g, lg_ss, lg_rs, late_per)
    near_out[pl.ds(early_g.shape[0], window), :] = late_g[...]
    sums_out[pl.ds(0, 8), :] = sums_t[...]
    for copy in tail_copies:
        copy.wait_recv()
    far_out[...] = tail_v[...]
    sums_out[pl.ds(8, 8), :] = tail_sums[...]

    for copy in halos + tail_copies:
        copy.wait_send()
    sends_wait(early_s, early_r, early_p, early_g, es_ss, es_rs, eg_ss, eg_rs, early_per)
    sends_wait(late_s, late_r, late_p, late_g, ls_ss, ls_rs, lg_ss, lg_rs, late_per)
    peers(lambda dist: sums_copy(dist).wait_send())


def reduced_sums(genotype, phenotype, residual, sign_flips, window):
    samples, snps = genotype.shape
    count, ring = lax.axis_size("samp"), lax.axis_size("snp")
    blocks = snps // window
    early_rows = (2 * blocks - 1) * window
    early_per, late_per = share_of(early_rows, count), share_of(window, count)
    half, wide = jnp.bfloat16, jnp.float32
    dma = pltpu.SemaphoreType.DMA
    vmem = pl.BlockSpec(memory_space=pltpu.VMEM)
    hbm = pl.BlockSpec(memory_space=pl.ANY)
    return pl.pallas_call(
        functools.partial(sums_kernel, count, ring, window),
        out_shape=(
            jax.ShapeDtypeStruct((2 * snps, window), half),
            jax.ShapeDtypeStruct((2 * window, window), half),
            jax.ShapeDtypeStruct((16, window), wide),
        ),
        in_specs=[hbm, vmem, vmem, hbm],
        out_specs=(vmem, vmem, vmem),
        scratch_shapes=[
            pltpu.VMEM((samples, snps), half),
            pltpu.VMEM(sign_flips.shape, jnp.int32),
            pltpu.VMEM((samples, window), half),
            pltpu.VMEM((samples, window), half),
            pltpu.VMEM((early_rows, window), half),
            pltpu.VMEM((count, early_per, window), half),
            pltpu.VMEM((early_per, window), half),
            pltpu.VMEM((early_rows, window), half),
            pltpu.VMEM((window, window), half),
            pltpu.VMEM((count, late_per, window), half),
            pltpu.VMEM((late_per, window), half),
            pltpu.VMEM((window, window), half),
            pltpu.VMEM((2 * window, window), half),
            pltpu.VMEM((8, window), wide),
            pltpu.VMEM((8, window), wide),
            pltpu.VMEM((count, 8, window), wide),
            pltpu.VMEM((8, window), wide),
            dma((PARTS,)), dma((PARTS,)), dma((PARTS,)), dma((PARTS,)),
            dma((count,)), dma((count,)), dma((count,)), dma((count,)),
            dma((count,)), dma((count,)), dma((count,)), dma((count,)),
            dma((count,)), dma((count,)), dma((2,)), dma((2,)),
        ],
        compiler_params=pltpu.CompilerParams(collective_id=0, has_side_effects=True),
        name="sums",
    )(genotype, phenotype.reshape(-1, window), residual.reshape(-1, window), sign_flips)


def scores_kernel(
    sample_total, offset_ref, start_ref, end_ref, near, far, sums, member, weights, out, placed,
):
    genes, tissues, window = weights.shape
    padded = placed.shape[0] // genes
    blocks = near.shape[0] // window // 2
    per_block = genes // blocks
    offset = offset_ref[0]
    row, col = iotas(window, window)
    inverse = 1.0 / sample_total

    all_sums = jnp.concatenate([sums[...], jnp.zeros((window - 16, window), jnp.float32)], axis=0)
    by_column = all_sums.T
    lab_sum = all_sums[blocks:blocks + 1]

    def mean_row(b):
        at = b if b < blocks else 8
        return all_sums[at:at + 1] * inverse

    def mean_col(b):
        at = b if b < blocks else 8
        return by_column[:, at:at + 1] * inverse

    def block_at(b, band):
        if b == blocks:
            at, ref = (1 if band else 0), far
        elif band:
            at, ref = (1 + b if b < blocks - 1 else 2 * blocks - 1), near
        else:
            at, ref = (0 if b == 0 else blocks + b - 1), near
        return ref[pl.ds(at * window, window), :].astype(jnp.float32)

    def with_labels(b):
        centred = block_at(b, False) - mean_col(b) * lab_sum
        centred = pltpu.roll(centred, 1, 1)
        high = centred.astype(jnp.bfloat16)
        low = (centred - high.astype(jnp.float32)).astype(jnp.bfloat16)
        return jnp.concatenate([high, low], axis=1)

    def diagonal(b):
        value = block_at(b, True) * inverse - mean_col(b) * mean_row(b)
        return jnp.where(col > row, 2.0 * value, jnp.where(col == row, value, 0.0))

    def beside(b):
        value = block_at(b, True) * inverse - mean_col(b) * mean_row(b + 1)
        return jnp.where(col < row, 2.0 * value, 0.0)

    member_cols = member[...].astype(jnp.float32).T
    pos = lax.broadcasted_iota(jnp.int32, (1, window), 1)
    for g in range(genes):
        b = g // per_block
        start, end = start_ref[g], end_ref[g]
        inside = (pos < end - start).astype(jnp.float32)
        values = weights[g].astype(jnp.float32) * member_cols[:, g:g + 1] * inside
        values = jnp.concatenate([values, jnp.zeros_like(values)], axis=1)
        shift = start - offset - b * window
        placed[pl.ds(g * padded, tissues), :] = pltpu.roll(values, shift, 1)

    root = 1.0 / (sample_total ** 0.5)
    labelled = [with_labels(b) for b in range(blocks + 1)]
    for b in range(blocks):
        pair = jnp.concatenate([labelled[b], labelled[b + 1]], axis=0)
        band = jnp.concatenate([
            jnp.concatenate([diagonal(b), beside(b)], axis=1),
            jnp.concatenate([jnp.zeros((window, window), jnp.float32), diagonal(b + 1)], axis=1),
        ], axis=0).astype(jnp.bfloat16)
        for g in range(b * per_block, (b + 1) * per_block, 2):
            wide = placed[pl.ds(g * padded, 2 * padded), :]
            half = wide.astype(jnp.bfloat16)
            top = jnp.dot(half, pair, preferred_element_type=jnp.float32)
            square = jnp.dot(half, band, preferred_element_type=jnp.float32)
            variance = jnp.sum(square * wide, axis=1, keepdims=True)
            scale = lax.rsqrt(jnp.maximum(variance, 0.0) + 1e-06) * root
            scores = (top[:, :window] + top[:, window:]) * scale
            out[g] = scores[0:tissues]
            out[g + 1] = scores[padded:padded + tissues]


def on_device(genotype, phenotype, residual, sign_flips, weights, member, gene_start, gene_end):
    samples, snps = genotype.shape
    genes, tissues, window = weights.shape
    near, far, sums = reduced_sums(genotype, phenotype, residual, sign_flips, window)
    offset = (lax.axis_index("snp") * snps).astype(jnp.int32).reshape(1)
    padded = -(-tissues // 8) * 8
    vmem = pl.BlockSpec(memory_space=pltpu.VMEM)
    smem = pl.BlockSpec(memory_space=pltpu.SMEM)
    return pl.pallas_call(
        functools.partial(scores_kernel, samples * lax.axis_size("samp")),
        out_shape=jax.ShapeDtypeStruct(weights.shape, jnp.float32),
        in_specs=[smem, smem, smem, vmem, vmem, vmem, vmem, vmem],
        out_specs=vmem,
        scratch_shapes=[pltpu.VMEM((genes * padded, 2 * window), jnp.float32)],
        name="scores",
    )(offset, gene_start, gene_end, near, far, sums, member, weights)


def solution(mesh):
    return jax.shard_map(
        on_device,
        mesh=mesh,
        in_specs=(
            P("samp", "snp"),
            P("samp"),
            P("samp"),
            P("samp", None),
            P("snp", None, None),
            P("snp", None),
            P("snp"),
            P("snp"),
        ),
        out_specs=P("snp", None, None),
        check_vma=False,
    )
```

```python
import functools

import jax
import jax.numpy as jnp
from jax import lax
from jax.experimental import pallas as pl
from jax.experimental.pallas import tpu as pltpu
from jax.sharding import PartitionSpec as P

MESH = pl.DeviceIdType.MESH
TILE = 16
PARTS = 4


def across(left, right):
    return lax.dot_general(left, right, (((0,), (0,)), ((), ())), preferred_element_type=jnp.float32)


def iotas(rows, cols):
    return (
        lax.broadcasted_iota(jnp.int32, (rows, cols), 0),
        lax.broadcasted_iota(jnp.int32, (rows, cols), 1),
    )


def share_of(rows, count):
    per = -(-rows // (count * TILE)) * TILE
    while rows % per:
        per += TILE
    return per


def columns_of(rows_ref):
    tiles, width = rows_ref.shape
    block = rows_ref[...]
    if tiles < width:
        block = jnp.concatenate([block, jnp.zeros((width - tiles, width), jnp.float32)], axis=0)
    return block.T


def sums_kernel(
    count, ring, window,
    geno, phen, resid, flips, starts, ends, member, weights,
    near_out, far_out, sums_out, corner_out, placed_out,
    geno_v, flips_v, halo_v, labels_v,
    early_s, early_r, early_p, early_g,
    late_s, late_r,
    tail_v, tail_sums, sums_s, sums_r, sums_t,
    load_sem, flip_sem, halo_ss, halo_rs,
    es_ss, es_rs, eg_ss, eg_rs, lt_ss, lt_rs,
    sm_ss, sm_rs, tl_ss, tl_rs,
):
    me = lax.axis_index("samp")
    mine = lax.axis_index("snp")
    before = lax.rem(mine + ring - 1, ring)
    after = lax.rem(mine + 1, ring)
    samples, snps = geno_v.shape
    blocks = snps // window
    part = samples // PARTS

    loads, flip_loads = [], []
    for i in range(PARTS):
        rows = pl.ds(i * part, part)
        loads.append(pltpu.make_async_copy(geno.at[rows], geno_v.at[rows], load_sem.at[i]))
        flip_loads.append(pltpu.make_async_copy(flips.at[rows], flips_v.at[rows], flip_sem.at[i]))
        loads[i].start()
        flip_loads[i].start()

    def peers(body):
        if count <= 16:
            for dist in range(1, count):
                body(dist)
        else:
            def step(dist, carry):
                body(dist)
                return carry
            lax.fori_loop(1, count, step, 0)

    def ahead(dist):
        return lax.rem(me + dist, count)

    def behind(dist):
        return lax.rem(me + count - dist, count)

    barrier = pltpu.get_barrier_semaphore()
    peers(lambda dist: pl.semaphore_signal(
        barrier, inc=1, device_id=(ahead(dist), mine), device_id_type=MESH))
    for other in (before, after):
        pl.semaphore_signal(barrier, inc=1, device_id=(me, other), device_id_type=MESH)

    flip_count = flips_v.shape[1]
    phen_cols = columns_of(phen)
    resid_cols = columns_of(resid)
    lanes = phen.shape[1]
    for i in range(PARTS):
        flip_loads[i].wait()
        for t in range(i * part // lanes, (i + 1) * part // lanes):
            rows = pl.ds(t * lanes, lanes)
            signs = flips_v[rows, :].astype(jnp.float32)
            labels_v[rows, pl.ds(0, flip_count)] = (signs * resid_cols[:, t:t + 1]).astype(jnp.bfloat16)
            labels_v[rows, pl.ds(flip_count, 1)] = phen_cols[:, t:t + 1].astype(jnp.bfloat16)

    pl.semaphore_wait(barrier, count + 1)

    def remote(src, dst, ss, rs, device):
        return pltpu.make_async_remote_copy(
            src_ref=src, dst_ref=dst, send_sem=ss, recv_sem=rs,
            device_id=device, device_id_type=MESH)

    halos = []
    for i in range(PARTS):
        rows = pl.ds(i * part, part)
        halos.append(remote(
            geno.at[rows, pl.ds(0, window)], halo_v.at[rows],
            halo_ss.at[i], halo_rs.at[i], (me, before)))
        halos[i].start()

    def guarded(owners, index, body):
        if owners == count:
            body()
        else:
            pl.when(index < owners)(body)

    def scatter_copy(buf, got, ss, rs, per, dist):
        start = pl.multiple_of(ahead(dist) * per, TILE)
        return remote(buf.at[pl.ds(start, per)], got.at[dist], ss.at[dist], rs.at[dist], (ahead(dist), mine))

    def gather_copy(piece, full, ss, rs, per, dist):
        start = pl.multiple_of(me * per, TILE)
        return remote(piece, full.at[pl.ds(start, per)], ss.at[dist], rs.at[dist], (ahead(dist), mine))

    def scatter_start(buf, got, ss, rs, per):
        owners = buf.shape[0] // per
        peers(lambda dist: guarded(
            owners, ahead(dist), lambda: scatter_copy(buf, got, ss, rs, per, dist).start()))

    def reduce_and_gather(buf, got, piece, full, ss, rs, gss, grs, per):
        owners = buf.shape[0] // per

        def owner():
            start = pl.multiple_of(me * per, TILE)
            rows = pl.ds(start, per)
            total = buf[rows, :].astype(jnp.float32)
            if count <= 16:
                for dist in range(1, count):
                    scatter_copy(buf, got, ss, rs, per, dist).wait_recv()
                    total += got[dist].astype(jnp.float32)
            else:
                def step(dist, total):
                    scatter_copy(buf, got, ss, rs, per, dist).wait_recv()
                    return total + got[dist].astype(jnp.float32)
                total = lax.fori_loop(1, count, step, total)
            piece[...] = total.astype(piece.dtype)
            peers(lambda dist: gather_copy(piece, full, gss, grs, per, dist).start())
            full[rows, :] = piece[...]
        guarded(owners, me, owner)

    def gather_wait(buf, piece, full, gss, grs, per):
        owners = buf.shape[0] // per

        def one(dist):
            start = pl.multiple_of(behind(dist) * per, TILE)
            guarded(owners, behind(dist), lambda: remote(
                piece, full.at[pl.ds(start, per)], gss.at[dist], grs.at[dist], (ahead(dist), mine)).wait_recv())
        peers(one)

    def sends_wait(buf, got, piece, full, ss, rs, gss, grs, per):
        owners = buf.shape[0] // per
        peers(lambda dist: guarded(
            owners, ahead(dist), lambda: scatter_copy(buf, got, ss, rs, per, dist).wait_send()))
        guarded(owners, me, lambda: peers(
            lambda dist: gather_copy(piece, full, gss, grs, per, dist).wait_send()))

    for i in range(PARTS):
        loads[i].wait()
    own = geno_v[...]
    labels = labels_v[...]
    with_labels = across(own, labels)
    gram = across(own, own)
    ones = jnp.ones((8, samples), jnp.bfloat16)
    col_sums = jnp.dot(ones, own, preferred_element_type=jnp.float32)
    lab_sums = jnp.dot(ones, labels, preferred_element_type=jnp.float32)
    row8, _ = iotas(8, window)
    sums = jnp.where(row8 == blocks, lab_sums, 0.0)
    for b in range(blocks):
        sums = jnp.where(row8 == b, col_sums[:, b * window:(b + 1) * window], sums)
    sums_s[...] = sums

    def sums_copy(dist):
        return remote(sums_s, sums_r.at[dist], sm_ss.at[dist], sm_rs.at[dist], (ahead(dist), mine))

    row, col = iotas(window, window)
    for b in range(blocks):
        low, mid, high = b * window, (b + 1) * window, (b + 2) * window
        beyond = gram[low:mid, mid:high] if b < blocks - 1 else 0.0
        early_s[pl.ds(2 * low, window), :] = with_labels[low:mid].astype(jnp.bfloat16)
        band = jnp.where(col >= row, gram[low:mid, low:mid], beyond)
        early_s[pl.ds(2 * low + window, window), :] = band.astype(jnp.bfloat16)
    early_per = early_p.shape[0]
    scatter_start(early_s, early_r, es_ss, es_rs, early_per)
    peers(lambda dist: sums_copy(dist).start())

    place(mine * snps, starts, ends, member, weights, placed_out)
    reduce_and_gather(early_s, early_r, early_p, early_g, es_ss, es_rs, eg_ss, eg_rs, early_per)

    last = snps - window
    corner = jnp.zeros((window, window), jnp.float32)
    for i in range(PARTS):
        rows = pl.ds(i * part, part)
        halos[i].wait_recv()
        corner += across(geno_v[rows, pl.ds(last, window)], halo_v[rows, :])
    mid = window // 2
    half_row, half_col = iotas(mid, window)
    turned = pltpu.roll(corner, mid, 1)[:mid]
    folded = jnp.where(half_col - mid > half_row, corner.T[mid:], turned)
    late_s[...] = jnp.where(half_col < mid, corner[mid:], folded).astype(jnp.bfloat16)

    def late_copy(dist):
        return remote(late_s, late_r.at[dist], lt_ss.at[dist], lt_rs.at[dist], (ahead(dist), mine))

    peers(lambda dist: late_copy(dist).start())

    def collect(make, got, total):
        if count <= 16:
            for dist in range(1, count):
                make(dist).wait_recv()
                total += got[dist].astype(jnp.float32)
            return total

        def step(dist, total):
            make(dist).wait_recv()
            return total + got[dist].astype(jnp.float32)
        return lax.fori_loop(1, count, step, total)

    sums_t[...] = collect(sums_copy, sums_r, sums_s[...])
    tail_copies = [remote(sums_t, tail_sums, tl_ss.at[0], tl_rs.at[0], (me, before))]
    tail_copies[0].start()
    gather_wait(early_s, early_p, early_g, eg_ss, eg_rs, early_per)
    tail_copies.append(remote(
        early_g.at[pl.ds(0, 2 * window)], tail_v, tl_ss.at[1], tl_rs.at[1], (me, before)))
    tail_copies[1].start()
    near_out[...] = early_g[...]
    sums_out[pl.ds(0, 8), :] = sums_t[...]

    folded = collect(late_copy, late_r, late_s[...].astype(jnp.float32))
    mirrored = jnp.concatenate([folded, folded], axis=0).T
    corner_out[pl.ds(0, mid), :] = pltpu.roll(folded, mid, 1)
    corner_out[pl.ds(mid, mid), :] = jnp.where(half_col < mid, folded, mirrored[mid:])

    for copy in tail_copies:
        copy.wait_recv()
    far_out[...] = tail_v[...]
    sums_out[pl.ds(8, 8), :] = tail_sums[...]

    for copy in halos + tail_copies:
        copy.wait_send()
    sends_wait(early_s, early_r, early_p, early_g, es_ss, es_rs, eg_ss, eg_rs, early_per)
    peers(lambda dist: sums_copy(dist).wait_send())
    peers(lambda dist: late_copy(dist).wait_send())


def place(offset, starts, ends, member, weights, placed):
    tissues, genes, window = weights.shape
    blocks = placed.shape[0]
    per_block = genes // blocks
    spacing = window // per_block
    gene_row, gene_col = iotas(genes, genes)

    def upright(row_ref):
        spread = jnp.broadcast_to(row_ref[...].astype(jnp.float32), (genes, genes))
        picked = jnp.where(gene_row == gene_col, spread, 0.0)
        return jnp.sum(picked, axis=1, keepdims=True).astype(jnp.int32)

    first, past = upright(starts), upright(ends)
    gene, lane = iotas(genes, window)
    inside = (lane < past - first).astype(jnp.float32)
    within = first - offset - (gene // per_block) * window
    extra = within - (gene % per_block) * spacing
    owned = member[...].astype(jnp.float32)
    for t in range(tissues):
        values = weights[t].astype(jnp.float32) * owned[:, t:t + 1] * inside
        bit = 1
        while bit < spacing:
            values = jnp.where((extra & bit) != 0, pltpu.roll(values, bit, 1), values)
            bit *= 2
        for b in range(blocks):
            genes_of = slice(b * per_block, (b + 1) * per_block)
            turned = pltpu.roll(values[genes_of], 0, 1, stride=spacing, stride_axis=0)
            kept = lane[genes_of] >= within[genes_of]
            rows = pl.ds(t * per_block, per_block)
            placed[b, rows, pl.ds(0, window)] = jnp.where(kept, turned, 0.0).astype(jnp.bfloat16)
            placed[b, rows, pl.ds(window, window)] = jnp.where(kept, 0.0, turned).astype(jnp.bfloat16)


def reduced_sums(genotype, phenotype, residual, sign_flips, starts, ends, member, weights):
    samples, snps = genotype.shape
    tissues, genes, window = weights.shape
    count, ring = lax.axis_size("samp"), lax.axis_size("snp")
    blocks = snps // window
    early_rows = 2 * snps
    early_per = share_of(early_rows, count)
    half, wide = jnp.bfloat16, jnp.float32
    dma = pltpu.SemaphoreType.DMA
    vmem = pl.BlockSpec(memory_space=pltpu.VMEM)
    hbm = pl.BlockSpec(memory_space=pl.ANY)
    return pl.pallas_call(
        functools.partial(sums_kernel, count, ring, window),
        out_shape=(
            jax.ShapeDtypeStruct((early_rows, window), half),
            jax.ShapeDtypeStruct((2 * window, window), half),
            jax.ShapeDtypeStruct((16, window), wide),
            jax.ShapeDtypeStruct((window, window), wide),
            jax.ShapeDtypeStruct((blocks, tissues * genes // blocks, 2 * window), half),
        ),
        in_specs=[hbm, vmem, vmem, hbm, vmem, vmem, vmem, vmem],
        out_specs=(vmem,) * 5,
        scratch_shapes=[
            pltpu.VMEM((samples, snps), half),
            pltpu.VMEM(sign_flips.shape, jnp.int32),
            pltpu.VMEM((samples, window), half),
            pltpu.VMEM((samples, window), half),
            pltpu.VMEM((early_rows, window), half),
            pltpu.VMEM((count, early_per, window), half),
            pltpu.VMEM((early_per, window), half),
            pltpu.VMEM((early_rows, window), half),
            pltpu.VMEM((window // 2, window), half),
            pltpu.VMEM((count, window // 2, window), half),
            pltpu.VMEM((2 * window, window), half),
            pltpu.VMEM((8, window), wide),
            pltpu.VMEM((8, window), wide),
            pltpu.VMEM((count, 8, window), wide),
            pltpu.VMEM((8, window), wide),
            dma((PARTS,)), dma((PARTS,)), dma((PARTS,)), dma((PARTS,)),
            dma((count,)), dma((count,)), dma((count,)), dma((count,)),
            dma((count,)), dma((count,)),
            dma((count,)), dma((count,)), dma((2,)), dma((2,)),
        ],
        compiler_params=pltpu.CompilerParams(collective_id=0, has_side_effects=True),
        name="sums",
    )(
        genotype, phenotype.reshape(-1, window), residual.reshape(-1, window), sign_flips,
        starts.reshape(1, genes), ends.reshape(1, genes), member, weights,
    )


def scores_kernel(sample_total, near, far, sums, corner, placed, out_hbm, out, sem):
    tissues, genes, window = out.shape
    blocks, rows_in_block, _ = placed.shape
    per_block = genes // blocks
    row, col = iotas(window, window)
    inverse = 1.0 / sample_total

    all_sums = jnp.concatenate([sums[...], jnp.zeros((window - 16, window), jnp.float32)], axis=0)
    by_column = all_sums.T
    lab_sum = all_sums[blocks:blocks + 1]

    def mean_row(b):
        at = b if b < blocks else 8
        return all_sums[at:at + 1] * inverse

    def mean_col(b):
        at = b if b < blocks else 8
        return by_column[:, at:at + 1] * inverse

    def block_at(b, band):
        ref, at = (near, 2 * b + band) if b < blocks else (far, band)
        return ref[pl.ds(at * window, window), :].astype(jnp.float32)

    def with_labels(b):
        centred = block_at(b, 0) - mean_col(b) * lab_sum
        centred = pltpu.roll(centred, 1, 1)
        high = centred.astype(jnp.bfloat16)
        low = (centred - high.astype(jnp.float32)).astype(jnp.bfloat16)
        return jnp.concatenate([high, low], axis=1)

    def diagonal(b):
        value = block_at(b, 1) * inverse - mean_col(b) * mean_row(b)
        return jnp.where(col > row, 2.0 * value, jnp.where(col == row, value, 0.0))

    def beside(b):
        products = block_at(b, 1) if b < blocks - 1 else corner[...]
        value = products * inverse - mean_col(b) * mean_row(b + 1)
        return jnp.where(col < row, 2.0 * value, 0.0)

    root = 1.0 / (sample_total ** 0.5)
    labelled = [with_labels(b) for b in range(blocks + 1)]
    pairs, bands = [], []
    for b in range(blocks):
        pairs.append(jnp.concatenate([labelled[b], labelled[b + 1]], axis=0))
        bands.append(jnp.concatenate([
            jnp.concatenate([diagonal(b), beside(b)], axis=1),
            jnp.concatenate([jnp.zeros((window, window), jnp.float32), diagonal(b + 1)], axis=1),
        ], axis=0).astype(jnp.bfloat16))

    copies = []
    step = next(n for n in range(min(7, tissues), 0, -1) if tissues % n == 0)
    for t in range(0, tissues, step):
        for b in range(blocks):
            half = placed[b, pl.ds(t * per_block, step * per_block), :]
            top = jnp.dot(half, pairs[b], preferred_element_type=jnp.float32)
            square = jnp.dot(half, bands[b], preferred_element_type=jnp.float32)
            variance = jnp.sum(square * half.astype(jnp.float32), axis=1, keepdims=True)
            scale = lax.rsqrt(jnp.maximum(variance, 0.0) + 1e-06) * root
            scores = (top[:, :window] + top[:, window:]) * scale
            out[pl.ds(t, step), pl.ds(b * per_block, per_block), :] = scores.reshape(step, per_block, window)
        part = pl.ds(t, step)
        copies.append(pltpu.make_async_copy(out.at[part], out_hbm.at[part], sem.at[t // step]))
        copies[-1].start()
    for copy in copies:
        copy.wait()


def on_device(genotype, phenotype, residual, sign_flips, weights, member, gene_start, gene_end):
    by_tissue = weights.transpose(1, 0, 2)
    near, far, sums, corner, placed = reduced_sums(
        genotype, phenotype, residual, sign_flips, gene_start, gene_end, member, by_tissue)
    vmem = pl.BlockSpec(memory_space=pltpu.VMEM)
    scores = pl.pallas_call(
        functools.partial(scores_kernel, genotype.shape[0] * lax.axis_size("samp")),
        out_shape=jax.ShapeDtypeStruct(by_tissue.shape, jnp.float32),
        in_specs=[vmem] * 5,
        out_specs=pl.BlockSpec(memory_space=pl.ANY),
        scratch_shapes=[
            pltpu.VMEM(by_tissue.shape, jnp.float32),
            pltpu.SemaphoreType.DMA((by_tissue.shape[0],)),
        ],
        name="scores",
    )(near, far, sums, corner, placed)
    return scores.transpose(1, 0, 2)


def solution(mesh):
    return jax.shard_map(
        on_device,
        mesh=mesh,
        in_specs=(
            P("samp", "snp"),
            P("samp"),
            P("samp"),
            P("samp", None),
            P("snp", None, None),
            P("snp", None),
            P("snp"),
            P("snp"),
        ),
        out_specs=P("snp", None, None),
        check_vma=False,
    )
```

```python
import functools

import jax
import jax.numpy as jnp
from jax import lax
from jax.experimental import pallas as pl
from jax.experimental.pallas import tpu as pltpu
from jax.sharding import PartitionSpec as P

MESH = pl.DeviceIdType.MESH
TILE = 16
PARTS = 4


def across(left, right):
    return lax.dot_general(left, right, (((0,), (0,)), ((), ())), preferred_element_type=jnp.float32)


def iotas(rows, cols):
    return (
        lax.broadcasted_iota(jnp.int32, (rows, cols), 0),
        lax.broadcasted_iota(jnp.int32, (rows, cols), 1),
    )


def share_of(rows, count):
    per = -(-rows // (count * TILE)) * TILE
    while rows % per:
        per += TILE
    return per


def columns_of(rows_ref):
    tiles, width = rows_ref.shape
    block = rows_ref[...]
    if tiles < width:
        block = jnp.concatenate([block, jnp.zeros((width - tiles, width), jnp.float32)], axis=0)
    return block.T


def sums_kernel(
    count, ring, window,
    geno, phen, resid, flips, starts, ends, member, weights,
    near_out, far_out, sums_out, corner_out, placed_hbm,
    geno_v, flips_v, halo_v, labels_v,
    early_s, early_r, early_p, early_g,
    late_s, late_r,
    weights_v, placed_v, tail_v, tail_sums, sums_s, sums_r, sums_t,
    load_sem, flip_sem, side_sem, halo_ss, halo_rs,
    es_ss, es_rs, eg_ss, eg_rs, lt_ss, lt_rs,
    sm_ss, sm_rs, tl_ss, tl_rs, fg_ss, fg_rs,
):
    me = lax.axis_index("samp")
    mine = lax.axis_index("snp")
    before = lax.rem(mine + ring - 1, ring)
    after = lax.rem(mine + 1, ring)
    samples, snps = geno_v.shape
    blocks = snps // window
    part = samples // PARTS

    loads, flip_loads = [], []
    for i in range(PARTS):
        rows = pl.ds(i * part, part)
        loads.append(pltpu.make_async_copy(geno.at[rows], geno_v.at[rows], load_sem.at[i]))
        flip_loads.append(pltpu.make_async_copy(flips.at[rows], flips_v.at[rows], flip_sem.at[i]))
        loads[i].start()
        flip_loads[i].start()

    weights_load = pltpu.make_async_copy(weights, weights_v, side_sem.at[0])
    weights_load.start()
    placed_save = pltpu.make_async_copy(placed_v, placed_hbm, side_sem.at[1])

    def peers(body):
        if count <= 16:
            for dist in range(1, count):
                body(dist)
        else:
            def step(dist, carry):
                body(dist)
                return carry
            lax.fori_loop(1, count, step, 0)

    def everyone(body):
        body(0)
        peers(body)

    def ahead(dist):
        return lax.rem(me + dist, count)

    def behind(dist):
        return lax.rem(me + count - dist, count)

    barrier = pltpu.get_barrier_semaphore()
    peers(lambda dist: pl.semaphore_signal(
        barrier, inc=1, device_id=(ahead(dist), mine), device_id_type=MESH))
    for other in (before, after):
        everyone(lambda dist: pl.semaphore_signal(
            barrier, inc=1, device_id=(ahead(dist), other), device_id_type=MESH))

    flip_count = flips_v.shape[1]
    phen_cols = columns_of(phen)
    resid_cols = columns_of(resid)
    lanes = phen.shape[1]
    for i in range(PARTS):
        flip_loads[i].wait()
        for t in range(i * part // lanes, (i + 1) * part // lanes):
            rows = pl.ds(t * lanes, lanes)
            signs = flips_v[rows, :].astype(jnp.float32)
            labels_v[rows, pl.ds(0, flip_count)] = (signs * resid_cols[:, t:t + 1]).astype(jnp.bfloat16)
            labels_v[rows, pl.ds(flip_count, 1)] = phen_cols[:, t:t + 1].astype(jnp.bfloat16)

    pl.semaphore_wait(barrier, 3 * count - 1)

    def remote(src, dst, ss, rs, device):
        return pltpu.make_async_remote_copy(
            src_ref=src, dst_ref=dst, send_sem=ss, recv_sem=rs,
            device_id=device, device_id_type=MESH)

    halos = []
    for i in range(PARTS):
        rows = pl.ds(i * part, part)
        halos.append(remote(
            geno.at[rows, pl.ds(0, window)], halo_v.at[rows],
            halo_ss.at[i], halo_rs.at[i], (me, before)))
        halos[i].start()

    def guarded(owners, index, body):
        if owners == count:
            body()
        else:
            pl.when(index < owners)(body)

    def scatter_copy(buf, got, ss, rs, per, dist):
        start = pl.multiple_of(ahead(dist) * per, TILE)
        return remote(buf.at[pl.ds(start, per)], got.at[dist], ss.at[dist], rs.at[dist], (ahead(dist), mine))

    def gather_copy(piece, full, ss, rs, per, dist):
        start = pl.multiple_of(me * per, TILE)
        return remote(piece, full.at[pl.ds(start, per)], ss.at[dist], rs.at[dist], (ahead(dist), mine))

    far_owners = tail_v.shape[0] // early_p.shape[0]

    def far_copy(dist):
        per = early_p.shape[0]
        start = pl.multiple_of(me * per, TILE)
        return remote(
            early_p, tail_v.at[pl.ds(start, per)], fg_ss.at[dist], fg_rs.at[dist], (ahead(dist), before))

    def far_wait(dist):
        per = early_p.shape[0]
        start = pl.multiple_of(behind(dist) * per, TILE)
        guarded(far_owners, behind(dist), lambda: remote(
            early_p, tail_v.at[pl.ds(start, per)], fg_ss.at[dist], fg_rs.at[dist],
            (ahead(dist), before)).wait_recv())

    def scatter_start(buf, got, ss, rs, per):
        owners = buf.shape[0] // per
        peers(lambda dist: guarded(
            owners, ahead(dist), lambda: scatter_copy(buf, got, ss, rs, per, dist).start()))

    def reduce_and_gather(buf, got, piece, full, ss, rs, gss, grs, per):
        owners = buf.shape[0] // per

        def owner():
            start = pl.multiple_of(me * per, TILE)
            rows = pl.ds(start, per)
            total = buf[rows, :].astype(jnp.float32)
            if count <= 16:
                for dist in range(1, count):
                    scatter_copy(buf, got, ss, rs, per, dist).wait_recv()
                    total += got[dist].astype(jnp.float32)
            else:
                def step(dist, total):
                    scatter_copy(buf, got, ss, rs, per, dist).wait_recv()
                    return total + got[dist].astype(jnp.float32)
                total = lax.fori_loop(1, count, step, total)
            piece[...] = total.astype(piece.dtype)
            peers(lambda dist: gather_copy(piece, full, gss, grs, per, dist).start())
            guarded(far_owners, me, lambda: everyone(lambda dist: far_copy(dist).start()))
            full[rows, :] = piece[...]
        guarded(owners, me, owner)

    def gather_wait(buf, piece, full, gss, grs, per):
        owners = buf.shape[0] // per

        def one(dist):
            start = pl.multiple_of(behind(dist) * per, TILE)
            guarded(owners, behind(dist), lambda: remote(
                piece, full.at[pl.ds(start, per)], gss.at[dist], grs.at[dist], (ahead(dist), mine)).wait_recv())
        peers(one)

    def sends_wait(buf, got, piece, full, ss, rs, gss, grs, per):
        owners = buf.shape[0] // per
        peers(lambda dist: guarded(
            owners, ahead(dist), lambda: scatter_copy(buf, got, ss, rs, per, dist).wait_send()))
        guarded(owners, me, lambda: peers(
            lambda dist: gather_copy(piece, full, gss, grs, per, dist).wait_send()))

    for i in range(PARTS):
        loads[i].wait()
    own = geno_v[...]
    labels = labels_v[...]
    with_labels = across(own, labels)
    gram = across(own, own)
    ones = jnp.ones((8, samples), jnp.bfloat16)
    col_sums = jnp.dot(ones, own, preferred_element_type=jnp.float32)
    lab_sums = jnp.dot(ones, labels, preferred_element_type=jnp.float32)
    row8, _ = iotas(8, window)
    sums = jnp.where(row8 == blocks, lab_sums, 0.0)
    for b in range(blocks):
        sums = jnp.where(row8 == b, col_sums[:, b * window:(b + 1) * window], sums)
    sums_s[...] = sums

    def sums_copy(dist):
        return remote(sums_s, sums_r.at[dist], sm_ss.at[dist], sm_rs.at[dist], (ahead(dist), mine))

    row, col = iotas(window, window)
    for b in range(blocks):
        low, mid, high = b * window, (b + 1) * window, (b + 2) * window
        beyond = gram[low:mid, mid:high] if b < blocks - 1 else 0.0
        early_s[pl.ds(2 * low, window), :] = with_labels[low:mid].astype(jnp.bfloat16)
        band = jnp.where(col >= row, gram[low:mid, low:mid], beyond)
        early_s[pl.ds(2 * low + window, window), :] = band.astype(jnp.bfloat16)
    early_per = early_p.shape[0]
    scatter_start(early_s, early_r, es_ss, es_rs, early_per)
    peers(lambda dist: sums_copy(dist).start())

    weights_load.wait()
    place(mine * snps, starts, ends, member, weights_v, placed_v)
    placed_save.start()
    reduce_and_gather(early_s, early_r, early_p, early_g, es_ss, es_rs, eg_ss, eg_rs, early_per)

    last = snps - window
    corner = jnp.zeros((window, window), jnp.float32)
    for i in range(PARTS):
        rows = pl.ds(i * part, part)
        halos[i].wait_recv()
        corner += across(geno_v[rows, pl.ds(last, window)], halo_v[rows, :])
    mid = window // 2
    half_row, half_col = iotas(mid, window)
    turned = pltpu.roll(corner, mid, 1)[:mid]
    folded = jnp.where(half_col - mid > half_row, corner.T[mid:], turned)
    late_s[...] = jnp.where(half_col < mid, corner[mid:], folded).astype(jnp.bfloat16)

    def late_copy(dist):
        return remote(late_s, late_r.at[dist], lt_ss.at[dist], lt_rs.at[dist], (ahead(dist), mine))

    peers(lambda dist: late_copy(dist).start())

    def collect(make, got, total):
        if count <= 16:
            for dist in range(1, count):
                make(dist).wait_recv()
                total += got[dist].astype(jnp.float32)
            return total

        def step(dist, total):
            make(dist).wait_recv()
            return total + got[dist].astype(jnp.float32)
        return lax.fori_loop(1, count, step, total)

    sums_t[...] = collect(sums_copy, sums_r, sums_s[...])
    tail_copies = [remote(sums_t, tail_sums, tl_ss.at[0], tl_rs.at[0], (me, before))]
    tail_copies[0].start()
    gather_wait(early_s, early_p, early_g, eg_ss, eg_rs, early_per)
    near_out[...] = early_g[...]
    sums_out[pl.ds(0, 8), :] = sums_t[...]

    folded = collect(late_copy, late_r, late_s[...].astype(jnp.float32))
    mirrored = jnp.concatenate([folded, folded], axis=0).T
    corner_out[pl.ds(0, mid), :] = pltpu.roll(folded, mid, 1)
    corner_out[pl.ds(mid, mid), :] = jnp.where(half_col < mid, folded, mirrored[mid:])

    for copy in tail_copies:
        copy.wait_recv()
    everyone(far_wait)
    far_out[...] = tail_v[...]
    sums_out[pl.ds(8, 8), :] = tail_sums[...]

    for copy in halos + tail_copies:
        copy.wait_send()
    sends_wait(early_s, early_r, early_p, early_g, es_ss, es_rs, eg_ss, eg_rs, early_per)
    peers(lambda dist: sums_copy(dist).wait_send())
    peers(lambda dist: late_copy(dist).wait_send())
    guarded(far_owners, me, lambda: everyone(lambda dist: far_copy(dist).wait_send()))
    placed_save.wait()


def place(offset, starts, ends, member, weights, placed):
    tissues, genes, window = weights.shape
    blocks = placed.shape[0]
    per_block = genes // blocks
    spacing = window // per_block
    gene_row, gene_col = iotas(genes, genes)

    def upright(row_ref):
        spread = jnp.broadcast_to(row_ref[...].astype(jnp.float32), (genes, genes))
        picked = jnp.where(gene_row == gene_col, spread, 0.0)
        return jnp.sum(picked, axis=1, keepdims=True).astype(jnp.int32)

    first, past = upright(starts), upright(ends)
    gene, lane = iotas(genes, window)
    inside = (lane < past - first).astype(jnp.float32)
    within = first - offset - (gene // per_block) * window
    extra = within - (gene % per_block) * spacing
    owned = member[...].astype(jnp.float32)
    for t in range(tissues):
        values = weights[t].astype(jnp.float32) * owned[:, t:t + 1] * inside
        bit = 1
        while bit < spacing:
            values = jnp.where((extra & bit) != 0, pltpu.roll(values, bit, 1), values)
            bit *= 2
        for b in range(blocks):
            genes_of = slice(b * per_block, (b + 1) * per_block)
            turned = pltpu.roll(values[genes_of], 0, 1, stride=spacing, stride_axis=0)
            kept = lane[genes_of] >= within[genes_of]
            rows = pl.ds(t * per_block, per_block)
            placed[b, rows, pl.ds(0, window)] = jnp.where(kept, turned, 0.0).astype(jnp.bfloat16)
            placed[b, rows, pl.ds(window, window)] = jnp.where(kept, 0.0, turned).astype(jnp.bfloat16)


def reduced_sums(genotype, phenotype, residual, sign_flips, starts, ends, member, weights):
    samples, snps = genotype.shape
    tissues, genes, window = weights.shape
    count, ring = lax.axis_size("samp"), lax.axis_size("snp")
    blocks = snps // window
    early_rows = 2 * snps
    early_per = share_of(early_rows, count)
    half, wide = jnp.bfloat16, jnp.float32
    dma = pltpu.SemaphoreType.DMA
    vmem = pl.BlockSpec(memory_space=pltpu.VMEM)
    hbm = pl.BlockSpec(memory_space=pl.ANY)
    return pl.pallas_call(
        functools.partial(sums_kernel, count, ring, window),
        out_shape=(
            jax.ShapeDtypeStruct((early_rows, window), half),
            jax.ShapeDtypeStruct((2 * window, window), half),
            jax.ShapeDtypeStruct((16, window), wide),
            jax.ShapeDtypeStruct((window, window), wide),
            jax.ShapeDtypeStruct((blocks, tissues * genes // blocks, 2 * window), half),
        ),
        in_specs=[hbm, vmem, vmem, hbm, vmem, vmem, vmem, hbm],
        out_specs=(vmem,) * 4 + (hbm,),
        scratch_shapes=[
            pltpu.VMEM((samples, snps), half),
            pltpu.VMEM(sign_flips.shape, jnp.int32),
            pltpu.VMEM((samples, window), half),
            pltpu.VMEM((samples, window), half),
            pltpu.VMEM((early_rows, window), half),
            pltpu.VMEM((count, early_per, window), half),
            pltpu.VMEM((early_per, window), half),
            pltpu.VMEM((early_rows, window), half),
            pltpu.VMEM((window // 2, window), half),
            pltpu.VMEM((count, window // 2, window), half),
            pltpu.VMEM(weights.shape, half),
            pltpu.VMEM((blocks, tissues * genes // blocks, 2 * window), half),
            pltpu.VMEM((2 * window, window), half),
            pltpu.VMEM((8, window), wide),
            pltpu.VMEM((8, window), wide),
            pltpu.VMEM((count, 8, window), wide),
            pltpu.VMEM((8, window), wide),
            dma((PARTS,)), dma((PARTS,)), dma((2,)), dma((PARTS,)), dma((PARTS,)),
            dma((count,)), dma((count,)), dma((count,)), dma((count,)),
            dma((count,)), dma((count,)),
            dma((count,)), dma((count,)), dma((1,)), dma((1,)),
            dma((count,)), dma((count,)),
        ],
        compiler_params=pltpu.CompilerParams(collective_id=0, has_side_effects=True),
        name="sums",
    )(
        genotype, phenotype.reshape(-1, window), residual.reshape(-1, window), sign_flips,
        starts.reshape(1, genes), ends.reshape(1, genes), member, weights,
    )


def scores_kernel(sample_total, near, far, sums, corner, placed, out_hbm, out, sem):
    tissues, genes, window = out.shape
    blocks, rows_in_block, _ = placed.shape
    per_block = genes // blocks
    row, col = iotas(window, window)
    inverse = 1.0 / sample_total

    all_sums = jnp.concatenate([sums[...], jnp.zeros((window - 16, window), jnp.float32)], axis=0)
    by_column = all_sums.T
    lab_sum = all_sums[blocks:blocks + 1]

    def mean_row(b):
        at = b if b < blocks else 8
        return all_sums[at:at + 1] * inverse

    def mean_col(b):
        at = b if b < blocks else 8
        return by_column[:, at:at + 1] * inverse

    def block_at(b, band):
        ref, at = (near, 2 * b + band) if b < blocks else (far, band)
        return ref[pl.ds(at * window, window), :].astype(jnp.float32)

    def with_labels(b):
        centred = block_at(b, 0) - mean_col(b) * lab_sum
        centred = pltpu.roll(centred, 1, 1)
        high = centred.astype(jnp.bfloat16)
        low = (centred - high.astype(jnp.float32)).astype(jnp.bfloat16)
        return jnp.concatenate([high, low], axis=1)

    def diagonal(b):
        value = block_at(b, 1) * inverse - mean_col(b) * mean_row(b)
        return jnp.where(col > row, 2.0 * value, jnp.where(col == row, value, 0.0))

    def beside(b):
        products = block_at(b, 1) if b < blocks - 1 else corner[...]
        value = products * inverse - mean_col(b) * mean_row(b + 1)
        return jnp.where(col < row, 2.0 * value, 0.0)

    root = 1.0 / (sample_total ** 0.5)
    labelled = [with_labels(b) for b in range(blocks + 1)]
    pairs, bands = [], []
    for b in range(blocks):
        pairs.append(jnp.concatenate([labelled[b], labelled[b + 1]], axis=0))
        bands.append(jnp.concatenate([
            jnp.concatenate([diagonal(b), beside(b)], axis=1),
            jnp.concatenate([jnp.zeros((window, window), jnp.float32), diagonal(b + 1)], axis=1),
        ], axis=0).astype(jnp.bfloat16))

    copies = []
    step = next(n for n in range(min(7, tissues), 0, -1) if tissues % n == 0)
    for t in range(0, tissues, step):
        for b in range(blocks):
            half = placed[b, pl.ds(t * per_block, step * per_block), :]
            top = jnp.dot(half, pairs[b], preferred_element_type=jnp.float32)
            square = jnp.dot(half, bands[b], preferred_element_type=jnp.float32)
            variance = jnp.sum(square * half.astype(jnp.float32), axis=1, keepdims=True)
            scale = lax.rsqrt(jnp.maximum(variance, 0.0) + 1e-06) * root
            scores = (top[:, :window] + top[:, window:]) * scale
            out[pl.ds(t, step), pl.ds(b * per_block, per_block), :] = scores.reshape(step, per_block, window)
        part = pl.ds(t, step)
        copies.append(pltpu.make_async_copy(out.at[part], out_hbm.at[part], sem.at[t // step]))
        copies[-1].start()
    for copy in copies:
        copy.wait()


def on_device(genotype, phenotype, residual, sign_flips, weights, member, gene_start, gene_end):
    by_tissue = weights.transpose(1, 0, 2)
    near, far, sums, corner, placed = reduced_sums(
        genotype, phenotype, residual, sign_flips, gene_start, gene_end, member, by_tissue)
    vmem = pl.BlockSpec(memory_space=pltpu.VMEM)
    scores = pl.pallas_call(
        functools.partial(scores_kernel, genotype.shape[0] * lax.axis_size("samp")),
        out_shape=jax.ShapeDtypeStruct(by_tissue.shape, jnp.float32),
        in_specs=[vmem] * 5,
        out_specs=pl.BlockSpec(memory_space=pl.ANY),
        scratch_shapes=[
            pltpu.VMEM(by_tissue.shape, jnp.float32),
            pltpu.SemaphoreType.DMA((by_tissue.shape[0],)),
        ],
        name="scores",
    )(near, far, sums, corner, placed)
    return scores.transpose(1, 0, 2)


def solution(mesh):
    return jax.shard_map(
        on_device,
        mesh=mesh,
        in_specs=(
            P("samp", "snp"),
            P("samp"),
            P("samp"),
            P("samp", None),
            P("snp", None, None),
            P("snp", None),
            P("snp"),
            P("snp"),
        ),
        out_specs=P("snp", None, None),
        check_vma=False,
    )
```

```python
import functools

import jax
import jax.numpy as jnp
from jax import lax
from jax.experimental import pallas as pl
from jax.experimental.pallas import tpu as pltpu
from jax.sharding import PartitionSpec as P

MESH = pl.DeviceIdType.MESH
TILE = 16
PARTS = 4


def across(left, right):
    return lax.dot_general(left, right, (((0,), (0,)), ((), ())), preferred_element_type=jnp.float32)


def iotas(rows, cols):
    return (
        lax.broadcasted_iota(jnp.int32, (rows, cols), 0),
        lax.broadcasted_iota(jnp.int32, (rows, cols), 1),
    )


def share_of(rows, count):
    per = -(-rows // (count * TILE)) * TILE
    while rows % per:
        per += TILE
    return per


def columns_of(rows_ref):
    tiles, width = rows_ref.shape
    block = rows_ref[...]
    if tiles < width:
        block = jnp.concatenate([block, jnp.zeros((width - tiles, width), jnp.float32)], axis=0)
    return block.T


def sums_kernel(
    count, ring, window,
    geno, phen, resid, flips, starts, ends, member, weights,
    near_out, far_out, sums_out, corner_out, placed_out,
    geno_v, flips_v, halo_v, labels_v,
    early_s, early_r, early_p, early_g,
    late_s, late_r,
    tail_v, tail_sums, sums_s, sums_r, sums_t,
    load_sem, flip_sem, halo_ss, halo_rs,
    es_ss, es_rs, eg_ss, eg_rs, lt_ss, lt_rs,
    sm_ss, sm_rs, tl_ss, tl_rs,
):
    me = lax.axis_index("samp")
    mine = lax.axis_index("snp")
    before = lax.rem(mine + ring - 1, ring)
    after = lax.rem(mine + 1, ring)
    samples, snps = geno_v.shape
    blocks = snps // window
    part = samples // PARTS

    loads, flip_loads = [], []
    for i in range(PARTS):
        rows = pl.ds(i * part, part)
        loads.append(pltpu.make_async_copy(geno.at[rows], geno_v.at[rows], load_sem.at[i]))
        flip_loads.append(pltpu.make_async_copy(flips.at[rows], flips_v.at[rows], flip_sem.at[i]))
        loads[i].start()
        flip_loads[i].start()

    def peers(body):
        if count <= 16:
            for dist in range(1, count):
                body(dist)
        else:
            def step(dist, carry):
                body(dist)
                return carry
            lax.fori_loop(1, count, step, 0)

    def ahead(dist):
        return lax.rem(me + dist, count)

    def behind(dist):
        return lax.rem(me + count - dist, count)

    barrier = pltpu.get_barrier_semaphore()
    peers(lambda dist: pl.semaphore_signal(
        barrier, inc=1, device_id=(ahead(dist), mine), device_id_type=MESH))
    for other in (before, after):
        pl.semaphore_signal(barrier, inc=1, device_id=(me, other), device_id_type=MESH)

    flip_count = flips_v.shape[1]
    phen_cols = columns_of(phen)
    resid_cols = columns_of(resid)
    lanes = phen.shape[1]
    for i in range(PARTS):
        flip_loads[i].wait()
        for t in range(i * part // lanes, (i + 1) * part // lanes):
            rows = pl.ds(t * lanes, lanes)
            signs = flips_v[rows, :].astype(jnp.float32)
            labels_v[rows, pl.ds(0, flip_count)] = (signs * resid_cols[:, t:t + 1]).astype(jnp.bfloat16)
            labels_v[rows, pl.ds(flip_count, 1)] = phen_cols[:, t:t + 1].astype(jnp.bfloat16)

    pl.semaphore_wait(barrier, count + 1)

    def remote(src, dst, ss, rs, device):
        return pltpu.make_async_remote_copy(
            src_ref=src, dst_ref=dst, send_sem=ss, recv_sem=rs,
            device_id=device, device_id_type=MESH)

    halos = []
    for i in range(PARTS):
        rows = pl.ds(i * part, part)
        halos.append(remote(
            geno.at[rows, pl.ds(0, window)], halo_v.at[rows],
            halo_ss.at[i], halo_rs.at[i], (me, before)))
        halos[i].start()

    def guarded(owners, index, body):
        if owners == count:
            body()
        else:
            pl.when(index < owners)(body)

    def scatter_copy(buf, got, ss, rs, per, dist):
        start = pl.multiple_of(ahead(dist) * per, TILE)
        return remote(buf.at[pl.ds(start, per)], got.at[dist], ss.at[dist], rs.at[dist], (ahead(dist), mine))

    def gather_copy(piece, full, ss, rs, per, dist):
        start = pl.multiple_of(me * per, TILE)
        return remote(piece, full.at[pl.ds(start, per)], ss.at[dist], rs.at[dist], (ahead(dist), mine))

    def scatter_start(buf, got, ss, rs, per):
        owners = buf.shape[0] // per
        peers(lambda dist: guarded(
            owners, ahead(dist), lambda: scatter_copy(buf, got, ss, rs, per, dist).start()))

    def reduce_and_gather(buf, got, piece, full, ss, rs, gss, grs, per):
        owners = buf.shape[0] // per

        def owner():
            start = pl.multiple_of(me * per, TILE)
            rows = pl.ds(start, per)
            total = buf[rows, :].astype(jnp.float32)
            if count <= 16:
                for dist in range(1, count):
                    scatter_copy(buf, got, ss, rs, per, dist).wait_recv()
                    total += got[dist].astype(jnp.float32)
            else:
                def step(dist, total):
                    scatter_copy(buf, got, ss, rs, per, dist).wait_recv()
                    return total + got[dist].astype(jnp.float32)
                total = lax.fori_loop(1, count, step, total)
            piece[...] = total.astype(piece.dtype)
            peers(lambda dist: gather_copy(piece, full, gss, grs, per, dist).start())
            full[rows, :] = piece[...]
        guarded(owners, me, owner)

    def gather_wait(piece, full, gss, grs, per, low, high):
        def one(dist):
            start = pl.multiple_of(behind(dist) * per, TILE)

            @pl.when((behind(dist) >= low) & (behind(dist) < high))
            def _():
                remote(
                    piece, full.at[pl.ds(start, per)], gss.at[dist], grs.at[dist],
                    (ahead(dist), mine)).wait_recv()
        peers(one)

    def sends_wait(buf, got, piece, full, ss, rs, gss, grs, per):
        owners = buf.shape[0] // per
        peers(lambda dist: guarded(
            owners, ahead(dist), lambda: scatter_copy(buf, got, ss, rs, per, dist).wait_send()))
        guarded(owners, me, lambda: peers(
            lambda dist: gather_copy(piece, full, gss, grs, per, dist).wait_send()))

    for i in range(PARTS):
        loads[i].wait()
    own = geno_v[...]
    labels = labels_v[...]
    with_labels = across(own, labels)
    gram = across(own, own)
    ones = jnp.ones((8, samples), jnp.bfloat16)
    col_sums = jnp.dot(ones, own, preferred_element_type=jnp.float32)
    lab_sums = jnp.dot(ones, labels, preferred_element_type=jnp.float32)
    row8, _ = iotas(8, window)
    sums = jnp.where(row8 == blocks, lab_sums, 0.0)
    for b in range(blocks):
        sums = jnp.where(row8 == b, col_sums[:, b * window:(b + 1) * window], sums)
    sums_s[...] = sums

    def sums_copy(dist):
        return remote(sums_s, sums_r.at[dist], sm_ss.at[dist], sm_rs.at[dist], (ahead(dist), mine))

    row, col = iotas(window, window)
    for b in range(blocks):
        low, mid, high = b * window, (b + 1) * window, (b + 2) * window
        beyond = gram[low:mid, mid:high] if b < blocks - 1 else 0.0
        early_s[pl.ds(2 * low, window), :] = with_labels[low:mid].astype(jnp.bfloat16)
        band = jnp.where(col >= row, gram[low:mid, low:mid], beyond)
        early_s[pl.ds(2 * low + window, window), :] = band.astype(jnp.bfloat16)
    early_per = early_p.shape[0]
    scatter_start(early_s, early_r, es_ss, es_rs, early_per)
    peers(lambda dist: sums_copy(dist).start())

    place(mine * snps, starts, ends, member, weights, placed_out)
    reduce_and_gather(early_s, early_r, early_p, early_g, es_ss, es_rs, eg_ss, eg_rs, early_per)

    last = snps - window
    corner = jnp.zeros((window, window), jnp.float32)
    for i in range(PARTS):
        rows = pl.ds(i * part, part)
        halos[i].wait_recv()
        corner += across(geno_v[rows, pl.ds(last, window)], halo_v[rows, :])
    mid = window // 2
    half_row, half_col = iotas(mid, window)
    turned = pltpu.roll(corner, mid, 1)[:mid]
    folded = jnp.where(half_col - mid > half_row, corner.T[mid:], turned)
    late_s[...] = jnp.where(half_col < mid, corner[mid:], folded).astype(jnp.bfloat16)

    def late_copy(dist):
        return remote(late_s, late_r.at[dist], lt_ss.at[dist], lt_rs.at[dist], (ahead(dist), mine))

    peers(lambda dist: late_copy(dist).start())

    def collect(make, got, total):
        if count <= 16:
            for dist in range(1, count):
                make(dist).wait_recv()
                total += got[dist].astype(jnp.float32)
            return total

        def step(dist, total):
            make(dist).wait_recv()
            return total + got[dist].astype(jnp.float32)
        return lax.fori_loop(1, count, step, total)

    sums_t[...] = collect(sums_copy, sums_r, sums_s[...])
    tail_copies = [remote(sums_t, tail_sums, tl_ss.at[0], tl_rs.at[0], (me, before))]
    tail_copies[0].start()
    first_owners = 2 * window // early_per
    gather_wait(early_p, early_g, eg_ss, eg_rs, early_per, 0, first_owners)
    tail_copies.append(remote(
        early_g.at[pl.ds(0, 2 * window)], tail_v, tl_ss.at[1], tl_rs.at[1], (me, before)))
    tail_copies[1].start()
    gather_wait(early_p, early_g, eg_ss, eg_rs, early_per, first_owners, early_s.shape[0] // early_per)
    near_out[...] = early_g[...]
    sums_out[pl.ds(0, 8), :] = sums_t[...]

    folded = collect(late_copy, late_r, late_s[...].astype(jnp.float32))
    mirrored = jnp.concatenate([folded, folded], axis=0).T
    corner_out[pl.ds(0, mid), :] = pltpu.roll(folded, mid, 1)
    corner_out[pl.ds(mid, mid), :] = jnp.where(half_col < mid, folded, mirrored[mid:])

    for copy in tail_copies:
        copy.wait_recv()
    far_out[...] = tail_v[...]
    sums_out[pl.ds(8, 8), :] = tail_sums[...]

    for copy in halos + tail_copies:
        copy.wait_send()
    sends_wait(early_s, early_r, early_p, early_g, es_ss, es_rs, eg_ss, eg_rs, early_per)
    peers(lambda dist: sums_copy(dist).wait_send())
    peers(lambda dist: late_copy(dist).wait_send())


def place(offset, starts, ends, member, weights, placed):
    tissues, genes, window = weights.shape
    blocks = placed.shape[0]
    per_block = genes // blocks
    spacing = window // per_block
    gene_row, gene_col = iotas(genes, genes)

    def upright(row_ref):
        spread = jnp.broadcast_to(row_ref[...].astype(jnp.float32), (genes, genes))
        picked = jnp.where(gene_row == gene_col, spread, 0.0)
        return jnp.sum(picked, axis=1, keepdims=True).astype(jnp.int32)

    first, past = upright(starts), upright(ends)
    gene, lane = iotas(genes, window)
    inside = (lane < past - first).astype(jnp.float32)
    within = first - offset - (gene // per_block) * window
    extra = within - (gene % per_block) * spacing
    owned = member[...].astype(jnp.float32)
    for t in range(tissues):
        values = weights[t].astype(jnp.float32) * owned[:, t:t + 1] * inside
        bit = 1
        while bit < spacing:
            values = jnp.where((extra & bit) != 0, pltpu.roll(values, bit, 1), values)
            bit *= 2
        for b in range(blocks):
            genes_of = slice(b * per_block, (b + 1) * per_block)
            turned = pltpu.roll(values[genes_of], 0, 1, stride=spacing, stride_axis=0)
            kept = lane[genes_of] >= within[genes_of]
            rows = pl.ds(t * per_block, per_block)
            placed[b, rows, pl.ds(0, window)] = jnp.where(kept, turned, 0.0).astype(jnp.bfloat16)
            placed[b, rows, pl.ds(window, window)] = jnp.where(kept, 0.0, turned).astype(jnp.bfloat16)


def reduced_sums(genotype, phenotype, residual, sign_flips, starts, ends, member, weights):
    samples, snps = genotype.shape
    tissues, genes, window = weights.shape
    count, ring = lax.axis_size("samp"), lax.axis_size("snp")
    blocks = snps // window
    early_rows = 2 * snps
    early_per = share_of(early_rows, count)
    half, wide = jnp.bfloat16, jnp.float32
    dma = pltpu.SemaphoreType.DMA
    vmem = pl.BlockSpec(memory_space=pltpu.VMEM)
    hbm = pl.BlockSpec(memory_space=pl.ANY)
    return pl.pallas_call(
        functools.partial(sums_kernel, count, ring, window),
        out_shape=(
            jax.ShapeDtypeStruct((early_rows, window), half),
            jax.ShapeDtypeStruct((2 * window, window), half),
            jax.ShapeDtypeStruct((16, window), wide),
            jax.ShapeDtypeStruct((window, window), wide),
            jax.ShapeDtypeStruct((blocks, tissues * genes // blocks, 2 * window), half),
        ),
        in_specs=[hbm, vmem, vmem, hbm, vmem, vmem, vmem, vmem],
        out_specs=(vmem,) * 5,
        scratch_shapes=[
            pltpu.VMEM((samples, snps), half),
            pltpu.VMEM(sign_flips.shape, jnp.int32),
            pltpu.VMEM((samples, window), half),
            pltpu.VMEM((samples, window), half),
            pltpu.VMEM((early_rows, window), half),
            pltpu.VMEM((count, early_per, window), half),
            pltpu.VMEM((early_per, window), half),
            pltpu.VMEM((early_rows, window), half),
            pltpu.VMEM((window // 2, window), half),
            pltpu.VMEM((count, window // 2, window), half),
            pltpu.VMEM((2 * window, window), half),
            pltpu.VMEM((8, window), wide),
            pltpu.VMEM((8, window), wide),
            pltpu.VMEM((count, 8, window), wide),
            pltpu.VMEM((8, window), wide),
            dma((PARTS,)), dma((PARTS,)), dma((PARTS,)), dma((PARTS,)),
            dma((count,)), dma((count,)), dma((count,)), dma((count,)),
            dma((count,)), dma((count,)),
            dma((count,)), dma((count,)), dma((2,)), dma((2,)),
        ],
        compiler_params=pltpu.CompilerParams(collective_id=0, has_side_effects=True),
        name="sums",
    )(
        genotype, phenotype.reshape(-1, window), residual.reshape(-1, window), sign_flips,
        starts.reshape(1, genes), ends.reshape(1, genes), member, weights,
    )


def scores_kernel(sample_total, near, far, sums, corner, placed, out_hbm, out, sem):
    tissues, genes, window = out.shape
    blocks, rows_in_block, _ = placed.shape
    per_block = genes // blocks
    row, col = iotas(window, window)
    inverse = 1.0 / sample_total

    all_sums = jnp.concatenate([sums[...], jnp.zeros((window - 16, window), jnp.float32)], axis=0)
    by_column = all_sums.T
    lab_sum = all_sums[blocks:blocks + 1]

    def mean_row(b):
        at = b if b < blocks else 8
        return all_sums[at:at + 1] * inverse

    def mean_col(b):
        at = b if b < blocks else 8
        return by_column[:, at:at + 1] * inverse

    def block_at(b, band):
        ref, at = (near, 2 * b + band) if b < blocks else (far, band)
        return ref[pl.ds(at * window, window), :].astype(jnp.float32)

    def with_labels(b):
        centred = block_at(b, 0) - mean_col(b) * lab_sum
        centred = pltpu.roll(centred, 1, 1)
        high = centred.astype(jnp.bfloat16)
        low = (centred - high.astype(jnp.float32)).astype(jnp.bfloat16)
        return jnp.concatenate([high, low], axis=1)

    def diagonal(b):
        value = block_at(b, 1) * inverse - mean_col(b) * mean_row(b)
        return jnp.where(col > row, 2.0 * value, jnp.where(col == row, value, 0.0))

    def beside(b):
        products = block_at(b, 1) if b < blocks - 1 else corner[...]
        value = products * inverse - mean_col(b) * mean_row(b + 1)
        return jnp.where(col < row, 2.0 * value, 0.0)

    root = 1.0 / (sample_total ** 0.5)
    labelled = [with_labels(b) for b in range(blocks + 1)]
    pairs, bands = [], []
    for b in range(blocks):
        pairs.append(jnp.concatenate([labelled[b], labelled[b + 1]], axis=0))
        bands.append(jnp.concatenate([
            jnp.concatenate([diagonal(b), beside(b)], axis=1),
            jnp.concatenate([jnp.zeros((window, window), jnp.float32), diagonal(b + 1)], axis=1),
        ], axis=0).astype(jnp.bfloat16))

    copies = []
    step = next(n for n in range(min(7, tissues), 0, -1) if tissues % n == 0)
    for t in range(0, tissues, step):
        for b in range(blocks):
            half = placed[b, pl.ds(t * per_block, step * per_block), :]
            top = jnp.dot(half, pairs[b], preferred_element_type=jnp.float32)
            square = jnp.dot(half, bands[b], preferred_element_type=jnp.float32)
            variance = jnp.sum(square * half.astype(jnp.float32), axis=1, keepdims=True)
            scale = lax.rsqrt(jnp.maximum(variance, 0.0) + 1e-06) * root
            scores = (top[:, :window] + top[:, window:]) * scale
            out[pl.ds(t, step), pl.ds(b * per_block, per_block), :] = scores.reshape(step, per_block, window)
        part = pl.ds(t, step)
        copies.append(pltpu.make_async_copy(out.at[part], out_hbm.at[part], sem.at[t // step]))
        copies[-1].start()
    for copy in copies:
        copy.wait()


def on_device(genotype, phenotype, residual, sign_flips, weights, member, gene_start, gene_end):
    by_tissue = weights.transpose(1, 0, 2)
    near, far, sums, corner, placed = reduced_sums(
        genotype, phenotype, residual, sign_flips, gene_start, gene_end, member, by_tissue)
    vmem = pl.BlockSpec(memory_space=pltpu.VMEM)
    scores = pl.pallas_call(
        functools.partial(scores_kernel, genotype.shape[0] * lax.axis_size("samp")),
        out_shape=jax.ShapeDtypeStruct(by_tissue.shape, jnp.float32),
        in_specs=[vmem] * 5,
        out_specs=pl.BlockSpec(memory_space=pl.ANY),
        scratch_shapes=[
            pltpu.VMEM(by_tissue.shape, jnp.float32),
            pltpu.SemaphoreType.DMA((by_tissue.shape[0],)),
        ],
        name="scores",
    )(near, far, sums, corner, placed)
    return scores.transpose(1, 0, 2)


def solution(mesh):
    return jax.shard_map(
        on_device,
        mesh=mesh,
        in_specs=(
            P("samp", "snp"),
            P("samp"),
            P("samp"),
            P("samp", None),
            P("snp", None, None),
            P("snp", None),
            P("snp"),
            P("snp"),
        ),
        out_specs=P("snp", None, None),
        check_vma=False,
    )
```
